32 devices in a mesh: expert: 8 (over y, x, core), dp: 4 (over z).
Axes of the slice: x: 2, y: 2, z: 4, core: 2. Of those that a mesh axis runs over, the one named last changes fastest.
Arguments:
- tokens: bfloat16 [4096, 2048], P(('expert', 'dp')), may hold values from -6 to 6
- expert_ids: int32 [4096, 4], P(('expert', 'dp')), may hold values from 0 to 15, all different within a row; in each aligned block of 128 rows (0 to 127, 128 to 255, ...) at most 96 rows name the same one
- gate_probs: float32 [4096, 4], P(('expert', 'dp')), may hold values from 0.05 to 0.5
- expert_weights: bfloat16 [2048, 3, 16, 384], P(None, None, 'expert'), may hold values from -0.125 to 0.125
- out_grad: bfloat16 [4096, 2048], P(('expert', 'dp')), may hold values from -1.5 to 1.5
Outputs:
- layer_out: bfloat16 [4096, 2048], P(('expert', 'dp'))
- token_grad: bfloat16 [4096, 2048], P(('expert', 'dp'))
- gate_grad: float32 [4096, 4], P(('expert', 'dp'))
- weight_grad: float32 [2048, 3, 16, 384], P('dp', None, 'expert')
The draws below stay inside these ranges and needn't reach their ends.
Inputs may be any that keep to these rules, and one draw needn't show every extreme that they name: `expert_ids`: each row names 4 different experts. Among the 128 rows of one device (aligned blocks of rows), no expert is named by more than 96 rows, and in some block some expert is named by exactly 96 rows.
All inputs are finite; a program needn't handle non-finite values.
Results may differ from the reference program's by a relative error of at most 0.0085.
Values may be sent and summed in bfloat16 or wider, within the bound.
A program may use at most 128 MiB of HBM per device.

```python
import math
import jax
import jax.numpy as jnp
import numpy as np
from jax import lax

D = 2048
H = 384
TOP = 4
TOK_DEV = 128
EXPERTS = 16
CAP = 96
TOKENS = 4096
N_DP = 4


def spiked(values, own_key, source, target, parts, factor):
    owner, partner = [(jnp.arange(values.shape[dim]) // (values.shape[dim] // parts)).reshape([-1 if axis == dim else 1 for axis in range(values.ndim)]) for dim in (source, target)]
    chosen = jax.random.permutation(own_key, parts)[partner]
    strong = (owner == chosen) | (owner == (partner + parts // 2) % parts)
    return jnp.where(strong, factor * values, values)


def block_scale(stream_key, shape, pieces, least, largest):
    def one(dim, parts):
        draws = jax.random.uniform(jax.random.fold_in(jax.random.fold_in(stream_key, 6), dim), (parts,), jnp.float32, least / len(pieces), largest / len(pieces))
        return jnp.repeat(jnp.exp(draws), shape[dim] // parts).reshape((-1,) + (1,) * (len(shape) - dim - 1))

    level = one(*pieces[0])
    for cut in pieces[1:]:
        level = level * one(*cut)
    return level


def assign_block(rng, own, number, rows, number_of, top, limit, lean):
    order = jax.random.permutation(rng, number_of)
    crowded, usual = shares(number_of, rows * top, limit, lean, True), shares(number_of, rows * top, limit, lean, False)
    places = jnp.arange(number_of)

    def named(tallies, rotation):
        used = int((tallies > 0).sum())
        fixed = max(1, used // 4)
        passed = fixed + (places - fixed + rotation * (used - fixed)) % max(1, number_of - fixed)
        return jnp.zeros((number_of,), jnp.int32).at[order[jnp.where(places < fixed, places, passed)]].set(jnp.asarray(tallies, jnp.int32))

    tallies = jnp.where(number % 4 == 0, named(crowded, number // 4), named(usual, number - number // 4 - 1))
    mixed = jax.random.permutation(jax.random.fold_in(own, 3), number_of)
    source_of, receiver = mixed[0:number_of // 2 * 2:2], mixed[1:number_of // 2 * 2:2]
    slack = jnp.minimum(tallies[source_of] - 1, limit - tallies[receiver]) // 2
    slack = jnp.where((source_of == order[0]) | (receiver == order[0]) | (tallies[receiver] == 0), 0, jnp.maximum(slack, 0))
    passed = jax.random.randint(jax.random.fold_in(own, 4), (number_of // 2,), 0, 1 << 20) % (slack + 1)
    tallies = tallies.at[source_of].add(-passed).at[receiver].add(passed)
    labels = jnp.searchsorted(jnp.cumsum(tallies), jnp.arange(rows * top), side="right").astype(jnp.int32)
    grid = labels.reshape(top, rows).T
    grid = grid[jax.random.permutation(jax.random.fold_in(own, 1), rows)]
    rotation = jax.random.randint(jax.random.fold_in(own, 2), (rows, 1), 0, top)
    return jnp.take_along_axis(grid, (jnp.arange(top)[None, :] + rotation) % top, axis=1)


def shares(number_of, total, bound, lean, full):
    weights = [(1 << 20) // math.isqrt(rank ** lean) + 1 for rank in range(1, number_of + 1)]
    largest = bound if full else min(bound, max(-(-total // number_of), total * weights[0] // sum(weights)))
    least = 1 if total - largest >= number_of - 1 else 0
    counts, rest = [largest] + [least] * (number_of - 1), total - largest - least * (number_of - 1)
    while rest > 0:
        free = [i for i in range(1, number_of) if counts[i] < largest] or [i for i in range(1, number_of) if counts[i] < bound]
        pool, left = sum([weights[i] for i in free]), rest
        for i in free:
            more = min(bound - counts[i], max(1, left * weights[i] // pool), rest)
            counts[i] = counts[i] + more
            rest = rest - more
    return np.array(counts)


def scatter_about(stream_key, dims, scale, most, cuts=(), kind=jnp.bfloat16):
    gain = block_scale(stream_key, dims, cuts, -0.22, 0.18) if cuts else 1.0
    values = jax.random.normal(stream_key, dims, jnp.float32) * scale * gain
    return jnp.minimum(jnp.maximum(values, -most), most).astype(kind)


def heavy_noise(rng, dims, width, limit, pieces, heavy, held_as=jnp.bfloat16):
    entries = width * jax.random.normal(rng, dims, jnp.float32)
    if pieces:
        entries = entries * block_scale(rng, dims, pieces, -0.22, 0.18)
    return jnp.clip(spiked(entries, jax.random.fold_in(rng, 3), *heavy), -limit, limit).astype(held_as)


def setup_inputs(seed: int = 0) -> dict:
    streams_of = jax.random.split(jax.random.key(seed), 6)
    tokens = heavy_noise(streams_of[0], (TOKENS, D), 1.0, 6.0, ((0, 32),), (0, 1, 32, 2.75))
    expert_ids_keys = jax.random.split(jax.random.fold_in(streams_of[1], 1), TOKENS // TOK_DEV)
    expert_ids_turns = jax.random.permutation(jax.random.fold_in(streams_of[1], 3), TOKENS // TOK_DEV)
    expert_ids = jax.vmap(lambda own, number: assign_block(jax.random.fold_in(streams_of[1], 2), own, number, TOK_DEV, EXPERTS, TOP, CAP, 2))(expert_ids_keys, expert_ids_turns).reshape((TOKENS, TOP))
    gate_probs = jnp.clip(0.05 + 0.45 * jax.random.uniform(streams_of[2], (TOKENS, TOP), jnp.float32) ** block_scale(streams_of[2], (TOKENS, TOP), ((0, 32),), -0.2, 0.2), 0.05, 0.5)
    expert_weights = scatter_about(streams_of[3], (D, 3, EXPERTS, H), D ** -0.5, 0.125, ((2, 8),))
    out_grad = scatter_about(streams_of[4], (TOKENS, D), 0.25, 1.5, ((0, 32),))
    return dict(tokens=tokens, expert_ids=expert_ids, gate_probs=gate_probs, expert_weights=expert_weights, out_grad=out_grad)


def rounded(values):
    return lax.optimization_barrier(values.astype(jnp.bfloat16)).astype(jnp.float32)


def reference(tokens, expert_ids, gate_probs, expert_weights, out_grad):
    tile_rows = 128
    pair_count = TOKENS * TOP
    key_count = EXPERTS * N_DP
    tile_count = pair_count // tile_rows + key_count
    pair_index = jnp.arange(pair_count, dtype=jnp.int32)
    pair_token = (pair_index // TOP).astype(jnp.int32)
    pair_expert = expert_ids.reshape(pair_count).astype(jnp.int32)
    pair_group = ((pair_token // TOK_DEV) % N_DP).astype(jnp.int32)
    pair_key = (pair_expert * N_DP + pair_group).astype(jnp.int32)
    key_sizes = jnp.zeros((key_count,), jnp.int32).at[pair_key].add(1)
    key_tiles = ((key_sizes + tile_rows - 1) // tile_rows).astype(jnp.int32)
    tile_first = (jnp.cumsum(key_tiles) - key_tiles).astype(jnp.int32)
    key_first = (jnp.cumsum(key_sizes) - key_sizes).astype(jnp.int32)
    ordering = jnp.argsort(pair_key, stable=True).astype(jnp.int32)
    sorted_key = pair_key[ordering]
    position = (tile_first[sorted_key] * tile_rows + pair_index - key_first[sorted_key]).astype(jnp.int32)
    slot_pair = jnp.full((tile_count * tile_rows,), -1, jnp.int32).at[position].set(ordering)
    tile_key = (jnp.searchsorted(tile_first, jnp.arange(tile_count, dtype=jnp.int32), side="right") - 1).astype(jnp.int32)
    flat_probs = gate_probs.reshape(pair_count)

    def step(carry, inputs):
        layer_acc, token_acc, gate_acc, group_acc, weight_acc, prev_key = carry
        slots, key_now = inputs
        filled = slots >= 0
        safe_pair = jnp.maximum(slots, 0)
        token_row = (safe_pair // TOP).astype(jnp.int32)
        expert_now = (key_now // N_DP).astype(jnp.int32)
        weight_now = lax.dynamic_index_in_dim(expert_weights, expert_now, axis=2, keepdims=False)
        row_block = jnp.where(filled[:, None], tokens[token_row], jnp.zeros((), jnp.bfloat16))
        gate_pre = jnp.dot(row_block, weight_now[:, 0], preferred_element_type=jnp.float32)
        up_pre = jnp.dot(row_block, weight_now[:, 1], preferred_element_type=jnp.float32)
        sigmoid_gate = jax.nn.sigmoid(gate_pre)
        hidden = (gate_pre * sigmoid_gate * up_pre).astype(jnp.bfloat16)
        output = jnp.dot(hidden, weight_now[:, 2].T, preferred_element_type=jnp.float32).astype(jnp.bfloat16)
        probs = jnp.where(filled, flat_probs[safe_pair], jnp.zeros((), jnp.float32))
        grad_block = out_grad[token_row]
        dump_token = jnp.where(filled, token_row, TOKENS)
        dump_pair = jnp.where(filled, safe_pair, pair_count)
        layer_acc = layer_acc.at[dump_token].add(probs[:, None] * output.astype(jnp.float32), mode="drop")
        gate_term = jnp.sum(grad_block.astype(jnp.float32) * output.astype(jnp.float32), axis=1)
        gate_acc = gate_acc.at[dump_pair].add(gate_term, mode="drop")
        out_cot = (probs[:, None] * grad_block.astype(jnp.float32)).astype(jnp.bfloat16)
        hidden_cot = jnp.dot(out_cot, weight_now[:, 2], preferred_element_type=jnp.float32)
        gate_cot = (hidden_cot * up_pre * sigmoid_gate * (1.0 + gate_pre * (1.0 - sigmoid_gate))).astype(jnp.bfloat16)
        up_cot = (hidden_cot * (gate_pre * sigmoid_gate)).astype(jnp.bfloat16)
        token_cot = (jnp.dot(gate_cot, weight_now[:, 0].T, preferred_element_type=jnp.float32)
                     + jnp.dot(up_cot, weight_now[:, 1].T, preferred_element_type=jnp.float32)).astype(jnp.bfloat16)
        token_acc = token_acc.at[dump_token].add(token_cot.astype(jnp.float32), mode="drop")
        tile_grad = jnp.stack([
            jnp.dot(row_block.T, gate_cot, preferred_element_type=jnp.float32),
            jnp.dot(row_block.T, up_cot, preferred_element_type=jnp.float32),
            jnp.dot(out_cot.T, hidden, preferred_element_type=jnp.float32)], axis=1)
        changed = key_now != prev_key
        prev_expert = (jnp.maximum(prev_key, 0) // N_DP).astype(jnp.int32)
        flushed = jnp.where(changed & (prev_key >= 0), rounded(group_acc), jnp.zeros((), jnp.float32))
        weight_acc = weight_acc.at[:, :, prev_expert].add(flushed)
        group_acc = jnp.where(changed, jnp.zeros((), jnp.float32), group_acc) + tile_grad
        return (layer_acc, token_acc, gate_acc, group_acc, weight_acc, key_now), None

    start = (jnp.zeros((TOKENS, D), jnp.float32), jnp.zeros((TOKENS, D), jnp.float32),
             jnp.zeros((pair_count,), jnp.float32), jnp.zeros((D, 3, H), jnp.float32),
             jnp.zeros((D, 3, EXPERTS, H), jnp.float32), jnp.array(-1, jnp.int32))
    final, unused = lax.scan(step, start, (slot_pair.reshape(tile_count, tile_rows), tile_key))
    layer_acc, token_acc, gate_acc, group_acc, weight_acc, prev_key = final
    last_expert = (jnp.maximum(prev_key, 0) // N_DP).astype(jnp.int32)
    weight_acc = weight_acc.at[:, :, last_expert].add(rounded(group_acc))
    return (layer_acc.astype(jnp.bfloat16), token_acc.astype(jnp.bfloat16),
            gate_acc.reshape(TOKENS, TOP), weight_acc)
```

```python
import jax
import jax.numpy as jnp
from jax import lax
from jax.sharding import PartitionSpec as P

F32 = jnp.float32
BF16 = jnp.bfloat16


def dot(a, b, ca, cb):
    return lax.dot_general(a, b, (((ca,), (cb,)), ((), ())), preferred_element_type=F32)


def local(tokens, expert_ids, gate_probs, expert_weights, out_grad):
    tok_count, top_count = expert_ids.shape
    d = tokens.shape[1]
    ranks = lax.axis_size("expert")
    me = lax.axis_index("expert")
    local_experts, h = expert_weights.shape[2:]
    n = ranks * tok_count
    eh = local_experts * h

    x = lax.all_gather(tokens, "expert", axis=0, tiled=True)
    small = jnp.concatenate([expert_ids.astype(F32), gate_probs], axis=1)
    small = lax.all_gather(small, "expert", axis=0, tiled=True)
    g = lax.all_gather(out_grad, "expert", axis=0, tiled=True)
    ids = small[:, :top_count].astype(jnp.int32)
    probs = small[:, top_count:]

    mine = me * local_experts + jnp.arange(local_experts, dtype=jnp.int32)
    hit = ids[:, :, None] == mine[None, None, :]
    p = jnp.sum(jnp.where(hit, probs[:, :, None], 0.0), axis=1)

    w = expert_weights.reshape(d, 3 * eh)
    wgu = w[:, : 2 * eh]
    wd = w[:, 2 * eh :]

    a = dot(x, wgu, 1, 0)
    gate = a[:, :eh].reshape(n, local_experts, h)
    up = a[:, eh:].reshape(n, local_experts, h)
    s = jax.nn.sigmoid(gate)
    hidden = gate * s * up
    ph = (p[:, :, None] * hidden).astype(BF16).reshape(n, eh)
    lpart = dot(ph, wd, 1, 1).astype(BF16)
    layer_out = lax.psum_scatter(lpart, "expert", scatter_dimension=0, tiled=True)

    wd_grad = dot(g, ph, 0, 0).astype(BF16)
    wd_grad = lax.psum_scatter(wd_grad, "dp", scatter_dimension=0, tiled=True)

    u = dot(g, wd, 1, 0).reshape(n, local_experts, h)
    gg = jnp.sum(u * hidden, axis=-1)
    hc = p[:, :, None] * u
    gc = (hc * up * s * (1.0 + gate * (1.0 - s))).astype(BF16).reshape(n, eh)
    uc = (hc * gate * s).astype(BF16).reshape(n, eh)
    cots = jnp.concatenate([gc, uc], axis=1)
    tpart = dot(cots, wgu, 1, 1).astype(BF16)
    token_grad = lax.psum_scatter(tpart, "expert", scatter_dimension=0, tiled=True)

    ggk = jnp.sum(jnp.where(hit, gg[:, None, :], 0.0), axis=2)
    gate_grad = lax.psum_scatter(ggk, "expert", scatter_dimension=0, tiled=True)

    wgu_grad = dot(x, cots, 0, 0).astype(BF16)
    wgu_grad = lax.psum_scatter(wgu_grad, "dp", scatter_dimension=0, tiled=True)
    wg = jnp.concatenate([wgu_grad, wd_grad], axis=1)
    weight_grad = wg.astype(F32).reshape(-1, 3, local_experts, h)
    return (layer_out, token_grad, gate_grad, weight_grad)


def solution(mesh):
    tok = P(("expert", "dp"), None)
    wsp = P(None, None, "expert", None)
    return jax.shard_map(
        local,
        mesh=mesh,
        in_specs=(tok, tok, tok, wsp, tok),
        out_specs=(tok, tok, tok, P("dp", None, "expert", None)),
        check_vma=False,
    )
```

```python
import jax
import jax.numpy as jnp
from jax import lax
from jax.sharding import Mesh, PartitionSpec as P

F32 = jnp.float32
BF16 = jnp.bfloat16
SWAP = [(0, 1), (1, 0)]


def dot(a, b, ca, cb):
    return lax.dot_general(a, b, (((ca,), (cb,)), ((), ())), preferred_element_type=F32)


def gather(rows):
    own = lax.all_gather(rows, "chip", axis=0, tiled=True)
    return own, lax.ppermute(own, "core", SWAP)


def scatter(own, other):
    total = own + lax.ppermute(other, "core", SWAP).astype(F32)
    return lax.psum_scatter(
        total.astype(other.dtype), "chip", scatter_dimension=0, tiled=True
    )


def line_scatter(grad):
    n = lax.axis_size("dp")
    me = lax.axis_index("dp")
    rows = grad.shape[0] // n

    def chunk(i):
        i = jnp.clip(i, 0, n - 1)
        return lax.dynamic_slice_in_dim(grad, i * rows, rows, 0).astype(F32)

    up = down = None
    for t in range(n - 1):
        a = chunk(n - 1 - t + me)
        b = chunk(t - (n - 1) + me)
        if t:
            a = a + up.astype(F32)
            b = b + down.astype(F32)
        up = lax.ppermute(a.astype(BF16), "dp", [(i, i + 1) for i in range(t + 1)])
        down = lax.ppermute(
            b.astype(BF16), "dp", [(i, i - 1) for i in range(n - 1 - t, n)]
        )
    return chunk(me) + up.astype(F32) + down.astype(F32)


def local(tokens, expert_ids, gate_probs, expert_weights, out_grad):
    tok_count, top_count = expert_ids.shape
    d = tokens.shape[1]
    chips = lax.axis_size("chip")
    core = lax.axis_index("core")
    me = lax.axis_index("chip") * 2 + core
    local_experts, h = expert_weights.shape[2:]
    half = chips * tok_count
    eh = local_experts * h

    x = jnp.concatenate(gather(tokens), axis=0)
    g = jnp.concatenate(gather(out_grad), axis=0)
    small = jnp.concatenate([expert_ids.astype(F32), gate_probs], axis=1)
    small = lax.all_gather(small, ("chip", "core"), axis=0)
    small = small.reshape(chips, 2, tok_count, 2 * top_count)
    small = jnp.where(core == 0, small, small[:, ::-1])
    small = small.transpose(1, 0, 2, 3).reshape(2 * half, 2 * top_count)
    ids = small[:, :top_count].astype(jnp.int32)
    probs = small[:, top_count:]

    hits = [ids == me * local_experts + i for i in range(local_experts)]
    p = jnp.concatenate(
        [
            jnp.broadcast_to(
                jnp.sum(jnp.where(hit, probs, 0.0), axis=1, keepdims=True), (2 * half, h)
            )
            for hit in hits
        ],
        axis=1,
    )

    w = expert_weights.reshape(d, 3 * eh)
    wgu = w[:, : 2 * eh]
    wd = w[:, 2 * eh :]

    a = dot(x, wgu, 1, 0)
    gate = a[:, :eh]
    up = a[:, eh:]
    s = jax.nn.sigmoid(gate)
    hidden = gate * s * up
    ph = (p * hidden).astype(BF16)
    down_grad = line_scatter(dot(g, ph, 0, 0).astype(BF16))

    u = dot(g, wd, 1, 0)
    hc = p * u
    gc = (hc * up * s * (1.0 + gate * (1.0 - s))).astype(BF16)
    uc = (hc * gate * s).astype(BF16)
    gate_part = line_scatter(dot(x, gc, 0, 0).astype(BF16))
    up_part = line_scatter(dot(x, uc, 0, 0).astype(BF16))

    other = dot(ph[half:], wd, 1, 1).astype(BF16)
    layer_out = scatter(dot(ph[:half], wd, 1, 1), other)

    cots = jnp.concatenate([gc, uc], axis=1)
    other = dot(cots[half:], wgu, 1, 1).astype(BF16)
    token_grad = scatter(dot(cots[:half], wgu, 1, 1), other)

    uh = u * hidden
    ggk = sum(
        jnp.where(hit, jnp.sum(uh[:, i * h : (i + 1) * h], axis=1, keepdims=True), 0.0)
        for i, hit in enumerate(hits)
    )
    gate_grad = scatter(ggk[:half], ggk[half:])

    weight_grad = jnp.stack([gate_part, up_part, down_grad], axis=1)
    weight_grad = weight_grad.reshape(-1, 3, local_experts, h)
    return (layer_out, token_grad, gate_grad, weight_grad)


def solution(mesh):
    experts, groups = mesh.devices.shape
    split = Mesh(
        mesh.devices.reshape(experts // 2, 2, groups), ("chip", "core", "dp")
    )
    tok = P(("chip", "core", "dp"), None)
    wsp = P(None, None, ("chip", "core"), None)
    return jax.shard_map(
        local,
        mesh=split,
        in_specs=(tok, tok, tok, wsp, tok),
        out_specs=(tok, tok, tok, P("dp", None, ("chip", "core"), None)),
        check_vma=False,
    )
```

```python
import jax
import jax.numpy as jnp
from jax import lax
from jax.sharding import Mesh, PartitionSpec as P

F32 = jnp.float32
BF16 = jnp.bfloat16
SWAP = [(0, 1), (1, 0)]


def dot(a, b, ca, cb):
    return lax.dot_general(a, b, (((ca,), (cb,)), ((), ())), preferred_element_type=F32)


def gather(rows):
    n = lax.axis_size("chip")
    own = [rows] + [
        lax.ppermute(rows, "chip", [(i, i ^ k) for i in range(n)]) for k in range(1, n)
    ]
    own = jnp.concatenate(own, axis=0)
    return jnp.concatenate([own, lax.ppermute(own, "core", SWAP)], axis=0)


def scatter(own, other):
    n = lax.axis_size("chip")
    me = lax.axis_index("chip")
    total = own + lax.ppermute(other, "core", SWAP).astype(F32)
    total = total.astype(other.dtype).reshape((n, -1) + own.shape[1:])
    total = jnp.concatenate(
        [lax.dynamic_index_in_dim(total, me ^ k, 0, keepdims=False) for k in range(n)],
        axis=0,
    )
    return lax.psum_scatter(total, "chip", scatter_dimension=0, tiled=True)


def line_scatter(grad):
    n = lax.axis_size("dp")
    me = lax.axis_index("dp")
    rows = grad.shape[0] // n

    def chunk(i):
        i = jnp.clip(i, 0, n - 1)
        return lax.dynamic_slice_in_dim(grad, i * rows, rows, 0).astype(F32)

    up = down = None
    for t in range(n - 1):
        a = chunk(n - 1 - t + me)
        b = chunk(t - (n - 1) + me)
        if t:
            a = a + up.astype(F32)
            b = b + down.astype(F32)
        up = lax.ppermute(a.astype(BF16), "dp", [(i, i + 1) for i in range(t + 1)])
        down = lax.ppermute(
            b.astype(BF16), "dp", [(i, i - 1) for i in range(n - 1 - t, n)]
        )
    return chunk(me) + up.astype(F32) + down.astype(F32)


def local(tokens, expert_ids, gate_probs, expert_weights, out_grad):
    tok_count, top_count = expert_ids.shape
    d = tokens.shape[1]
    chips = lax.axis_size("chip")
    me = lax.axis_index("chip") * 2 + lax.axis_index("core")
    local_experts, h = expert_weights.shape[2:]
    half = chips * tok_count
    eh = local_experts * h

    x = gather(tokens)
    small = gather(jnp.concatenate([expert_ids.astype(F32), gate_probs], axis=1))
    g = gather(out_grad)
    ids = small[:, :top_count].astype(jnp.int32)
    probs = small[:, top_count:]

    hits = [ids == me * local_experts + i for i in range(local_experts)]
    p = jnp.concatenate(
        [
            jnp.broadcast_to(
                jnp.sum(jnp.where(hit, probs, 0.0), axis=1, keepdims=True), (2 * half, h)
            )
            for hit in hits
        ],
        axis=1,
    )

    w = expert_weights.reshape(d, 3 * eh)
    wgu = w[:, : 2 * eh]
    wd = w[:, 2 * eh :]

    a = dot(x, wgu, 1, 0)
    gate = a[:, :eh]
    up = a[:, eh:]
    s = jax.nn.sigmoid(gate)
    hidden = gate * s * up
    ph = (p * hidden).astype(BF16)
    down_grad = line_scatter(dot(g, ph, 0, 0).astype(BF16))

    u = dot(g, wd, 1, 0)
    hc = p * u
    gc = (hc * up * s * (1.0 + gate * (1.0 - s))).astype(BF16)
    uc = (hc * gate * s).astype(BF16)
    gate_part = line_scatter(dot(x, gc, 0, 0).astype(BF16))
    up_part = line_scatter(dot(x, uc, 0, 0).astype(BF16))

    other = dot(ph[half:], wd, 1, 1).astype(BF16)
    layer_out = scatter(dot(ph[:half], wd, 1, 1), other)

    cots = jnp.concatenate([gc, uc], axis=1)
    other = dot(cots[half:], wgu, 1, 1).astype(BF16)
    token_grad = scatter(dot(cots[:half], wgu, 1, 1), other)

    uh = u * hidden
    ggk = sum(
        jnp.where(hit, jnp.sum(uh[:, i * h : (i + 1) * h], axis=1, keepdims=True), 0.0)
        for i, hit in enumerate(hits)
    )
    gate_grad = scatter(ggk[:half], ggk[half:])

    weight_grad = jnp.stack([gate_part, up_part, down_grad], axis=1)
    weight_grad = weight_grad.reshape(-1, 3, local_experts, h)
    return (layer_out, token_grad, gate_grad, weight_grad)


def solution(mesh):
    experts, groups = mesh.devices.shape
    split = Mesh(
        mesh.devices.reshape(experts // 2, 2, groups), ("chip", "core", "dp")
    )
    tok = P(("chip", "core", "dp"), None)
    wsp = P(None, None, ("chip", "core"), None)
    return jax.shard_map(
        local,
        mesh=split,
        in_specs=(tok, tok, tok, wsp, tok),
        out_specs=(tok, tok, tok, P("dp", None, ("chip", "core"), None)),
        check_vma=False,
    )
```
